32 devices in a mesh: gx: 8 (over y, x, core), gy: 4 (over z).
Axes of the slice: x: 2, y: 2, z: 4, core: 2. Of those that a mesh axis runs over, the one named last changes fastest.
Arguments:
- source: float32 [160, 80, 640], P('gx', 'gy'), may hold values from -210 to 210
- conductivity: float32 [160, 80, 640], P('gx', 'gy'), may hold values from 0.001 to 1
- absorption: float32 [160, 80, 640], P('gx', 'gy'), may hold values from 1 to 10
Outputs:
- solution: float32 [160, 80, 640], P('gx', 'gy')
- correction: float32 [96, 48, 384], P('gx', 'gy')
The draws below stay inside these ranges and needn't reach their ends.
All inputs are finite; a program needn't handle non-finite values.
Results may differ from the reference program's by a relative error of at most 0.00023.
Values sent between devices are 32-bit elements; how exact they have to be, the bound alone decides.
A program may use at most 128 MiB of HBM per device.

```python
import math
import jax
import jax.numpy as jnp
import numpy as np
from jax import lax

SWEEPS = 3
NX = 160
NY = 80
NZ = 640


def draw_source(key, part):
    first = jax.random.fold_in(key, 0)
    shape = (NX, NY, NZ)
    rise_x = 3.0 ** (jnp.arange(NX, dtype=jnp.float32) / NX)
    rise_y = 3.0 ** (jnp.arange(NY, dtype=jnp.float32) / NY)
    ramp = rise_x[:, None, None] * rise_y[None, :, None]
    base = jax.random.truncated_normal(first, -4.0, 4.0, shape, jnp.float32)
    return (base * ramp).astype(jnp.float32)


def draw_conductivity(key, part):
    inner = jax.random.fold_in(key, 17)
    shape = (NX, NY, NZ)
    place_x = jnp.arange(NX, dtype=jnp.float32) / NX
    place_y = jnp.arange(NY, dtype=jnp.float32) / NY
    rise_x = 10.0 ** place_x / 10.0
    base = jnp.exp(jax.random.uniform(inner, shape, jnp.float32, math.log(0.1), 0.0))
    rise_y = 3.0 ** place_y / 3.0
    ramp = rise_x[:, None, None] * rise_y[None, :, None]
    return (base * ramp).astype(jnp.float32)


def levels(stream_key, dims, cuts, low, largest):
    gain, own = 1.0, jax.random.fold_in(stream_key, 6)
    for position, blocks in cuts:
        steps = jnp.exp(jax.random.uniform(jax.random.fold_in(own, position), (blocks,), jnp.float32, low / len(cuts), largest / len(cuts)))
        gain = gain * jnp.repeat(steps, dims[position] // blocks).reshape([-1 if axis == position else 1 for axis in range(len(dims))])
    return gain


def setup_inputs(seed: int = 0) -> dict:
    splits = jax.random.split(jax.random.key(seed), 4)
    return {
        "source": draw_source(jax.random.fold_in(splits[3], 71), 0),
        "conductivity": draw_conductivity(jax.random.fold_in(splits[3], 71), 0),
        "absorption": jnp.clip(jnp.exp(math.log(10.0) - 2.3025851 * jax.random.uniform(splits[2], (NX, NY, NZ), jnp.float32) ** levels(splits[2], (NX, NY, NZ), ((0, 8), (1, 4)), -0.2, 0.2)), 1.0, 10.0),
    }


HIGH = lax.Precision.HIGHEST

def deriv_table(points):
    count = len(points)
    barycentric = np.array([1.0 / np.prod([points[j] - points[k] for k in range(count) if k != j]) for j in range(count)])
    table = np.zeros((count, count))
    for i in range(count):
        for j in range(count):
            if i != j:
                table[i, j] = barycentric[j] / (barycentric[i] * (points[i] - points[j]))
        table[i, i] = -np.sum(table[i])
    return table

def make_tables():
    root = math.sqrt(3.0 / 7.0)
    fine_points = np.array([-1.0, -root, 0.0, root, 1.0])
    fine_weights = np.array([0.1, 49.0 / 90.0, 32.0 / 45.0, 49.0 / 90.0, 0.1])
    coarse_points = np.array([-1.0, 0.0, 1.0])
    coarse_weights = np.array([1.0 / 3.0, 4.0 / 3.0, 1.0 / 3.0])
    interp = np.stack([fine_points * (fine_points - 1.0) / 2.0, 1.0 - fine_points ** 2, fine_points * (fine_points + 1.0) / 2.0], 1)
    select = np.zeros((3, 5))
    select[0, 0] = 1.0
    select[1, 2] = 1.0
    select[2, 4] = 1.0
    return [jnp.asarray(t, jnp.float32) for t in (fine_weights, coarse_weights, deriv_table(fine_points), deriv_table(coarse_points), interp, select)]

def along(field, table, axis):
    count_out, count_in = table.shape
    shape = field.shape
    elems = shape[axis] // count_in
    split = field.reshape(shape[:axis] + (elems, count_in) + shape[axis + 1:])
    moved = jnp.moveaxis(split, axis + 1, -1)
    mixed = jnp.einsum('...i,pi->...p', moved, table, precision=HIGH)
    back = jnp.moveaxis(mixed, -1, axis + 1)
    return back.reshape(shape[:axis] + (elems * count_out,) + shape[axis + 1:])

def end_masks(length, count, axis):
    index = jnp.arange(length) % count
    shape = [1, 1, 1]
    shape[axis] = length
    return ((index == 0).reshape(shape), (index == count - 1).reshape(shape))

def assemble(field, count):
    for axis in range(3):
        lower, upper = end_masks(field.shape[axis], count, axis)
        field = field + jnp.where(upper, jnp.roll(field, -1, axis), 0.0) + jnp.where(lower, jnp.roll(field, 1, axis), 0.0)
    return field

def node_weights(shape, weights):
    count = weights.shape[0]
    first = jnp.tile(weights, shape[0] // count)
    second = jnp.tile(weights, shape[1] // count)
    third = jnp.tile(weights, shape[2] // count)
    return first[:, None, None] * second[None, :, None] * third[None, None, :]

def half_ends(shape, count):
    parts = []
    for axis in range(3):
        lower, upper = end_masks(shape[axis], count, axis)
        parts.append(jnp.where(lower | upper, 0.5, 1.0))
    return parts[0] * parts[1] * parts[2]

def local_op(field, flux, mass, deriv):
    result = mass * field
    for axis in range(3):
        result = result + along(flux * along(field, deriv, axis), deriv.T, axis)
    return result

def local_diag(flux, mass, deriv):
    result = mass
    square = (deriv * deriv).T
    for axis in range(3):
        result = result + along(flux, square, axis)
    return result

def chebyshev(rhs, apply, inverse, estimate, want_residual):
    theta = 0.75 * estimate
    delta = 0.45 * estimate
    sigma = 5.0 / 3.0
    rho = 0.6
    solution = jnp.zeros_like(rhs)
    residual = rhs
    direction = inverse * residual / theta
    for sweep in range(SWEEPS):
        solution = solution + direction
        if sweep + 1 < SWEEPS or want_residual:
            residual = residual - apply(direction)
        if sweep + 1 < SWEEPS:
            rho_next = 1.0 / (2.0 * sigma - rho)
            direction = rho_next * rho * direction + 2.0 * rho_next / delta * inverse * residual
            rho = rho_next
    return (solution, residual)

def estimate_of(start, apply, inverse):
    first = inverse * apply(start)
    second = inverse * apply(first)
    return jnp.sqrt(jnp.sum(second * second) / (jnp.sum(first * first) + 1e-06))

def reference(source, conductivity, absorption):
    fine_weights, coarse_weights, fine_deriv, coarse_deriv, interp, select = make_tables()
    fine_w = node_weights(source.shape, fine_weights)
    fine_flux = fine_w * conductivity
    fine_mass = fine_w * absorption

    def apply_fine(field):
        return assemble(local_op(field, fine_flux, fine_mass, fine_deriv), 5)
    load = assemble(fine_w * source, 5)
    fine_inverse = 1.0 / assemble(local_diag(fine_flux, fine_mass, fine_deriv), 5)
    fine_estimate = estimate_of(load, apply_fine, fine_inverse)
    smoothed, fine_residual = chebyshev(load, apply_fine, fine_inverse, fine_estimate, True)
    coarse_cond = conductivity
    coarse_abs = absorption
    for axis in range(3):
        coarse_cond = along(coarse_cond, select, axis)
        coarse_abs = along(coarse_abs, select, axis)
    coarse_w = node_weights(coarse_cond.shape, coarse_weights)
    coarse_flux = coarse_w * coarse_cond
    coarse_mass = coarse_w * coarse_abs
    halves = half_ends(source.shape, 5)

    def apply_coarse(field):
        return assemble(local_op(field, coarse_flux, coarse_mass, coarse_deriv), 3)

    def restrict(field):
        field = field * halves
        for axis in range(3):
            field = along(field, interp.T, axis)
        return assemble(field, 3)
    coarse_inverse = 1.0 / assemble(local_diag(coarse_flux, coarse_mass, coarse_deriv), 3)
    coarse_estimate = estimate_of(restrict(load), apply_coarse, coarse_inverse)
    correction, unused = chebyshev(restrict(fine_residual), apply_coarse, coarse_inverse, coarse_estimate, False)
    lifted = correction
    for axis in range(3):
        lifted = along(lifted, interp, axis)
    return (smoothed + lifted, correction)
```

```python
import functools
import math

import jax
import jax.numpy as jnp
import numpy as np
from jax import lax
from jax.experimental import pallas as pl
from jax.experimental.pallas import tpu as pltpu
from jax.sharding import PartitionSpec as P

SWEEPS = 3
STAGES = 7
MESH = pl.DeviceIdType.MESH
DIRS = [(-1, 0), (1, 0), (0, -1), (0, 1), (-1, -1), (-1, 1), (1, -1), (1, 1)]


def deriv_table(points):
    count = len(points)
    barycentric = np.array(
        [
            1.0 / np.prod([points[j] - points[k] for k in range(count) if k != j])
            for j in range(count)
        ]
    )
    table = np.zeros((count, count))
    for i in range(count):
        for j in range(count):
            if i != j:
                table[i, j] = barycentric[j] / (barycentric[i] * (points[i] - points[j]))
        table[i, i] = -np.sum(table[i])
    return table


ROOT = math.sqrt(3.0 / 7.0)
FINE_POINTS = np.array([-1.0, -ROOT, 0.0, ROOT, 1.0])
FINE_W = np.array([0.1, 49.0 / 90.0, 32.0 / 45.0, 49.0 / 90.0, 0.1])
COARSE_POINTS = np.array([-1.0, 0.0, 1.0])
COARSE_W = np.array([1.0 / 3.0, 4.0 / 3.0, 1.0 / 3.0])
FINE_D = deriv_table(FINE_POINTS)
COARSE_D = deriv_table(COARSE_POINTS)
INTERP = np.stack(
    [
        FINE_POINTS * (FINE_POINTS - 1.0) / 2.0,
        1.0 - FINE_POINTS**2,
        FINE_POINTS * (FINE_POINTS + 1.0) / 2.0,
    ],
    1,
)
RESTRICT = INTERP.T * np.array([0.5, 1.0, 1.0, 1.0, 0.5])[None, :]
QF, QC = 5, 3


def chebyshev_coefficients():
    theta, delta, sigma, rho = 0.75, 0.45, 5.0 / 3.0, 0.6
    x = np.zeros(SWEEPS + 1)
    r = np.zeros(SWEEPS + 1)
    r[0] = 1.0
    d = r / theta
    for sweep in range(SWEEPS):
        x = x + d
        r = r - np.concatenate([[0.0], d[:-1]])
        if sweep + 1 < SWEEPS:
            rho_next = 1.0 / (2.0 * sigma - rho)
            d = rho_next * rho * d + 2.0 * rho_next / delta * r
            rho = rho_next
    return [float(v) for v in x[:SWEEPS]]


CHEB = chebyshev_coefficients()


def antisym(table, u):
    n = len(u)
    half = n // 2
    even = [u[j] + u[n - 1 - j] for j in range(half)]
    odd = [u[j] - u[n - 1 - j] for j in range(half)]
    out = [None] * n
    for i in range(half):
        p = float(table[i, half]) * u[half]
        q = None
        for j in range(half):
            s = (table[i, j] + table[i, n - 1 - j]) / 2
            t = (table[i, j] - table[i, n - 1 - j]) / 2
            p = p + float(s) * even[j]
            q = float(t) * odd[j] if q is None else q + float(t) * odd[j]
        out[i] = q + p
        out[n - 1 - i] = q - p
    mid = None
    for j in range(half):
        term = float(table[half, j]) * odd[j]
        mid = term if mid is None else mid + term
    out[half] = mid
    return out


def dense(table, u):
    out = []
    for i in range(table.shape[0]):
        acc = None
        for j in range(table.shape[1]):
            c = float(table[i, j])
            if abs(c) < 1e-14:
                continue
            term = u[j] if c == 1.0 else c * u[j]
            acc = term if acc is None else acc + term
        out.append(acc)
    return out


def plane_starts(q, axis, a, b):
    strides = (q * q, q, 1)
    other = [s for k, s in enumerate(strides) if k != axis]
    return a * other[0] + b * other[1], strides[axis]


def z_sum(line, lanes):
    lo, hi = line[0], line[-1]
    line[-1] = hi + pltpu.roll(lo, lanes - 1, 1)
    line[0] = lo + pltpu.roll(hi, 1, 1)
    return line


def local_op(src, dst, flux, mass, table, lanes):
    q = table.shape[0]
    for axis in range(3):

        @pl.loop(0, q)
        def _(a, axis=axis):
            for b in range(q):
                start, step = plane_starts(q, axis, a, b)
                u = [src[start + step * i] for i in range(q)]
                g = antisym(table, u)
                g = [flux[start + step * i] * g[i] for i in range(q)]
                r = antisym(table.T, g)
                for i in range(q):
                    base = mass[start + step * i] * u[i] if axis == 0 else dst[start + step * i]
                    r[i] = base + r[i]
                if axis == 2:
                    r = z_sum(r, lanes)
                for i in range(q):
                    dst[start + step * i] = r[i]


def local_diag(dst, flux, mass, table, lanes):
    q = table.shape[0]
    square = (table * table).T
    for axis in range(3):

        @pl.loop(0, q)
        def _(a, axis=axis):
            for b in range(q):
                start, step = plane_starts(q, axis, a, b)
                r = dense(square, [flux[start + step * i] for i in range(q)])
                for i in range(q):
                    base = mass if axis == 0 else dst
                    r[i] = base[start + step * i] + r[i]
                if axis == 2:
                    r = z_sum(r, lanes)
                for i in range(q):
                    dst[start + step * i] = r[i]


def kernel(
    nx,
    ny,
    src_ref,
    cond_ref,
    abs_ref,
    out_ref,
    cor_ref,
    wide,
    raw,
    craw,
    perm,
    back,
    cback,
    fine,
    flux,
    mass,
    coarse,
    cflux,
    cmass,
    tmp_a,
    tmp_b,
    send,
    recv,
    line_x_send,
    line_x,
    line_y_send,
    line_y,
    send_sem,
    recv_sem,
    line_send_sem,
    line_x_sem,
    line_y_sem,
):
    px, py, pz = src_ref.shape
    ex, ey, ez = px // QF, py // QF, pz // QF
    subs, lanes = ex * ey, ez
    rows_x = -(-py // 8) * 8
    rows = px * rows_x
    mx, my = lax.axis_index("gx"), lax.axis_index("gy")

    def target(dx, dy):
        return (lax.rem(mx + dx + nx, nx), lax.rem(my + dy + ny, ny))

    greeted = {(o, 0) for o in range(1, nx)} | {(0, o) for o in range(1, ny)}
    greeted |= {(dx % nx, dy % ny) for dx, dy in DIRS}
    greeted = sorted(greeted)
    barrier = pltpu.get_barrier_semaphore()
    for dx, dy in greeted:
        pl.semaphore_signal(barrier, inc=1, device_id=target(dx, dy), device_id_type=MESH)

    sub = lax.broadcasted_iota(jnp.int32, (subs, lanes), 0)

    def any_of(indices):
        mask = None
        for index in indices:
            one = sub == index
            mask = one if mask is None else mask | one
        return mask

    x_group = [(sub >= j * ey) & (sub < (j + 1) * ey) for j in range(ex)]
    y_group = [any_of([e * ey + j for e in range(ex)]) for j in range(ey)]
    at_sub = {}

    def single(index):
        if index not in at_sub:
            at_sub[index] = sub == index
        return at_sub[index]

    def shifted(plane, shift):
        shift = shift % subs
        return plane if shift == 0 else pltpu.roll(plane, shift, 0)

    def layout(d):
        dx, dy = DIRS[d]
        if dy == 0:
            return ex, ey, (0 if dx < 0 else ex - 1), (ex - 1 if dx < 0 else 0)
        if dx == 0:
            return ey, 1, (0 if dy < 0 else ey - 1), (ey - 1 if dy < 0 else 0)
        sx, tx = (0, ex - 1) if dx < 0 else (ex - 1, 0)
        sy, ty = (0, ey - 1) if dy < 0 else (ey - 1, 0)
        return subs, 1, sx * ey + sy, tx * ey + ty

    def group_mask(d, j):
        dx, dy = DIRS[d]
        if dy == 0:
            return x_group[j]
        if dx == 0:
            return y_group[j]
        return single(j)

    def face_planes(d, q):
        dx, dy = DIRS[d]
        xs = range(q) if dx == 0 else [0 if dx < 0 else q - 1]
        ys = range(q) if dy == 0 else [0 if dy < 0 else q - 1]
        return [(x * q + y) * q + z for x in xs for y in ys for z in range(q)]

    def copy_of(stage, d, tiles):
        return pltpu.make_async_remote_copy(
            src_ref=send.at[stage, d, pl.ds(0, tiles)],
            dst_ref=recv.at[stage, d, pl.ds(0, tiles)],
            send_sem=send_sem.at[stage, d],
            recv_sem=recv_sem.at[stage, d],
            device_id=target(*DIRS[d]),
            device_id_type=MESH,
        )

    pending = []

    def start_exchange(stage, fields):
        copies = []
        for d in range(len(DIRS)):
            groups, distance, source, _ = layout(d)
            planes = [ref.at[p] for ref, q in fields for p in face_planes(d, q)]
            tiles = -(-len(planes) // groups)
            for t in range(tiles):
                acc = None
                for j, plane in enumerate(planes[t * groups : (t + 1) * groups]):
                    moved = shifted(plane[...], (j - source) * distance)
                    acc = moved if acc is None else jnp.where(group_mask(d, j), moved, acc)
                send[stage, d, t] = acc
            copy = copy_of(stage, d, tiles)
            copy.start()
            copies.append(copy)
        return copies

    not_first_x, not_last_x = sub >= ey, sub < (ex - 1) * ey
    first_y, last_y = y_group[0], y_group[ey - 1]

    def finish_exchange(stage, fields, copies):
        for copy in copies:
            copy.wait_recv()
        pending.extend(copies)

        def received(d, number):
            groups, distance, _, place = layout(d)
            tile, j = divmod(number, groups)
            return shifted(recv[stage, d, tile], (place - j) * distance)

        offsets = [0] * len(DIRS)
        for ref, q in fields:
            last = q - 1
            plane = lambda x, y, z: (x * q + y) * q + z

            def x_sum(lo, hi, from_low, from_high):
                new_lo = lo + jnp.where(not_first_x, shifted(hi, ey), from_low)
                new_hi = hi + jnp.where(not_last_x, shifted(lo, -ey), from_high)
                return new_lo, new_hi

            for y in range(q):
                for z in range(q):
                    number = y * q + z
                    lo, hi = x_sum(
                        ref[plane(0, y, z)],
                        ref[plane(last, y, z)],
                        received(1, offsets[1] + number),
                        received(0, offsets[0] + number),
                    )
                    ref[plane(0, y, z)] = lo
                    ref[plane(last, y, z)] = hi
            for z in range(q):
                low = [received(3, offsets[3] + x * q + z) for x in range(q)]
                high = [received(2, offsets[2] + x * q + z) for x in range(q)]
                low[0], low[last] = x_sum(
                    low[0], low[last], received(7, offsets[7] + z), received(5, offsets[5] + z)
                )
                high[0], high[last] = x_sum(
                    high[0], high[last], received(6, offsets[6] + z), received(4, offsets[4] + z)
                )
                for x in range(q):
                    lo, hi = ref[plane(x, 0, z)], ref[plane(x, last, z)]
                    ref[plane(x, 0, z)] = lo + jnp.where(first_y, low[x], shifted(hi, 1))
                    ref[plane(x, last, z)] = hi + jnp.where(last_y, high[x], shifted(lo, -1))
            for d in range(len(DIRS)):
                offsets[d] += len(face_planes(d, q))

    def start_line(which, along_x, first, second):
        out, slots, sems = (
            (line_x_send, line_x, line_x_sem) if along_x else (line_y_send, line_y, line_y_sem)
        )
        count = nx if along_x else ny
        out[which, 0:1] = first
        out[which, 1:2] = second
        copies = []
        for o in range(1, count):
            copy = pltpu.make_async_remote_copy(
                src_ref=out.at[which],
                dst_ref=slots.at[which, o],
                send_sem=line_send_sem.at[which, 0 if along_x else 1, o],
                recv_sem=sems.at[which, o],
                device_id=target(o, 0) if along_x else target(0, o),
                device_id_type=MESH,
            )
            copy.start()
            copies.append(copy)
        return copies

    def finish_line(which, along_x, copies):
        out, slots = (line_x_send, line_x) if along_x else (line_y_send, line_y)
        count = nx if along_x else ny
        for copy in copies:
            copy.wait_recv()
        pending.extend(copies)
        total = out[which]
        for o in range(1, count):
            total = total + slots[which, o]
        return total[0:1], total[1:2]

    def inverse_estimate(first, second):
        first = jnp.sum(first, axis=1, keepdims=True)
        second = jnp.sum(second, axis=1, keepdims=True)
        return 1.0 / jnp.sqrt(second / (first + 1e-06))

    def coefficients(inv_est):
        power = inv_est
        out = []
        for c in CHEB:
            out.append(jnp.broadcast_to(c * power, (subs, lanes)))
            power = power * inv_est
        return out

    for k in range(QF):
        row = lax.broadcasted_iota(jnp.int32, (pz, ez), 0)
        col = lax.broadcasted_iota(jnp.int32, (pz, ez), 1)
        perm[:, k * ez : (k + 1) * ez] = jnp.where(row == QF * col + k, 1.0, 0.0).astype(
            jnp.bfloat16
        )

    def transposed_permutation(ref, q):
        for k in range(q):
            row = lax.broadcasted_iota(jnp.int32, (ez, q * ez), 0)
            col = lax.broadcasted_iota(jnp.int32, (ez, q * ez), 1)
            ref[k * ez : (k + 1) * ez, :] = jnp.where(col == q * row + k, 1.0, 0.0).astype(
                jnp.bfloat16
            )

    def split_dot(value, table):
        high = value.astype(jnp.bfloat16)
        rest = value - high.astype(jnp.float32)
        mid = rest.astype(jnp.bfloat16)
        low = (rest - mid.astype(jnp.float32)).astype(jnp.bfloat16)
        dot = functools.partial(jnp.dot, preferred_element_type=jnp.float32)
        return dot(high, table) + (dot(mid, table) + dot(low, table))

    for n, ref in enumerate((src_ref, cond_ref, abs_ref)):
        for x in range(px):
            wide[n * rows + x * rows_x : n * rows + x * rows_x + py, :] = ref[x]
    chunk = rows // 2

    @pl.loop(0, 6)
    def _(c):
        at = pl.multiple_of(c * chunk, 8)
        moved = split_dot(wide[pl.ds(at, chunk), :], perm[...])
        for k in range(QF):
            raw[k, pl.ds(at, chunk), :] = moved[:, k * ez : (k + 1) * ez]

    pick = {0: 0, 2: 1, 4: 2}
    for x in range(QF):
        for y in range(QF):
            for z in range(QF):
                p = (x * QF + y) * QF + z
                weight = float(FINE_W[x] * FINE_W[y] * FINE_W[z])
                on_coarse = x in pick and y in pick and z in pick
                for e in range(ex):
                    at = (e * QF + x) * rows_x + y
                    values = [
                        raw[z, pl.ds(n * rows + at, ey, stride=QF), :] for n in range(3)
                    ]
                    place = slice(e * ey, (e + 1) * ey)
                    fine[0, p, place, :] = weight * values[0]
                    flux[p, place, :] = weight * values[1]
                    mass[p, place, :] = weight * values[2]
                    if on_coarse:
                        i, j, k = pick[x], pick[y], pick[z]
                        cp = (i * QC + j) * QC + k
                        cw = float(COARSE_W[i] * COARSE_W[j] * COARSE_W[k])
                        cflux[cp, place, :] = cw * values[1]
                        cmass[cp, place, :] = cw * values[2]

    load, inv, power, w0, w1, w2, b = [fine.at[i] for i in range(7)]
    power_2 = fine.at[7]
    cinv, cur, crhs, cw0, cb, cpow, cw1, ccor = [coarse.at[i] for i in range(8)]

    def each(q, body):
        @pl.loop(0, q * q)
        def _(a):
            for i in range(q):
                body(a * q + i)

    def squares(q, values):
        def body(a, acc):
            for i in range(q):
                v = values(a * q + i)
                acc = acc + v * v
            return acc

        total = lax.fori_loop(0, q * q, body, jnp.zeros((subs, lanes), jnp.float32))
        return jnp.sum(total, axis=0, keepdims=True)

    def store(dst, values):
        def body(p):
            dst[p] = values(p)

        return body

    def restrict(field, dst):
        for x in range(1):

            @pl.loop(0, QF)
            def _(a):
                for c in range(QF):
                    line = dense(RESTRICT, [field[i * QF * QF + a * QF + c] for i in range(QF)])
                    for i in range(QC):
                        tmp_a[i * QF * QF + a * QF + c] = line[i]

        @pl.loop(0, QC)
        def _(a):
            for c in range(QF):
                line = dense(RESTRICT, [tmp_a[a * QF * QF + i * QF + c] for i in range(QF)])
                for i in range(QC):
                    tmp_b[a * QC * QF + i * QF + c] = line[i]

        @pl.loop(0, QC)
        def _(a):
            for c in range(QC):
                line = dense(RESTRICT, [tmp_b[a * QC * QF + c * QF + i] for i in range(QF)])
                line = z_sum(line, lanes)
                for i in range(QC):
                    dst[a * QC * QC + c * QC + i] = line[i]

    def apply_fine(src, dst):
        local_op(src, dst, flux, mass, FINE_D, lanes)

    def apply_coarse(src, dst):
        local_op(src, dst, cflux, cmass, COARSE_D, lanes)

    @pl.loop(0, QF * QF)
    def _(a):
        line = z_sum([load[a * QF + i] for i in range(QF)], lanes)
        load[a * QF] = line[0]
        load[a * QF + QF - 1] = line[-1]

    local_diag(inv, flux, mass, FINE_D, lanes)
    local_diag(cinv, cflux, cmass, COARSE_D, lanes)
    pl.semaphore_wait(barrier, len(greeted))
    fields = [(load, QF), (inv, QF), (cinv, QC)]
    copies = start_exchange(0, fields)
    transposed_permutation(back, QF)
    transposed_permutation(cback, QC)
    finish_exchange(0, fields, copies)

    def invert(p):
        value = 1.0 / inv[p]
        inv[p] = value
        b[p] = value * load[p]

    each(QF, invert)
    each(QC, store(cinv, lambda p: 1.0 / cinv[p]))

    apply_fine(load, power)
    apply_fine(b, w0)
    restrict(load, crhs)
    fields = [(power, QF), (w0, QF), (crhs, QC)]
    finish_exchange(1, fields, start_exchange(1, fields))
    each(QF, store(power, lambda p: inv[p] * power[p]))
    each(QF, store(b, lambda p: inv[p] * w0[p]))

    apply_fine(power, power_2)
    apply_fine(b, w1)
    apply_coarse(crhs, cpow)
    fields = [(power_2, QF), (w1, QF), (cpow, QC)]
    copies = start_exchange(2, fields)
    sum_first = squares(QF, lambda p: power[p])
    finish_exchange(2, fields, copies)
    sum_second = squares(QF, lambda p: inv[p] * power_2[p])
    line = start_line(0, True, sum_first, sum_second)
    each(QF, store(b, lambda p: inv[p] * w1[p]))
    each(QC, store(cpow, lambda p: cinv[p] * cpow[p]))

    apply_fine(b, w2)
    line = start_line(0, False, *finish_line(0, True, line))
    apply_coarse(cpow, cur)
    fields = [(w2, QF), (cur, QC)]
    copies = start_exchange(3, fields)
    csum_first = squares(QC, lambda p: cpow[p])
    scale = coefficients(inverse_estimate(*finish_line(0, False, line)))
    finish_exchange(3, fields, copies)
    csum_second = squares(QC, lambda p: cinv[p] * cur[p])
    each(
        QF,
        store(
            b, lambda p: load[p] - (scale[0] * w0[p] + scale[1] * w1[p] + scale[2] * w2[p])
        ),
    )

    restrict(b, crhs)
    fields = [(crhs, QC)]
    copies = start_exchange(4, fields)
    line = start_line(1, True, csum_first, csum_second)
    each(
        QF,
        store(
            power,
            lambda p: inv[p] * (scale[0] * load[p] + scale[1] * w0[p] + scale[2] * w1[p]),
        ),
    )
    finish_exchange(4, fields, copies)
    each(QC, store(cb, lambda p: cinv[p] * crhs[p]))

    apply_coarse(cb, cw0)
    fields = [(cw0, QC)]
    copies = start_exchange(5, fields)
    line = start_line(1, False, *finish_line(1, True, line))
    finish_exchange(5, fields, copies)
    each(QC, store(cb, lambda p: cinv[p] * cw0[p]))

    apply_coarse(cb, cw1)
    fields = [(cw1, QC)]
    copies = start_exchange(6, fields)
    cscale = coefficients(inverse_estimate(*finish_line(1, False, line)))
    finish_exchange(6, fields, copies)
    each(
        QC,
        store(
            ccor,
            lambda p: cinv[p]
            * (cscale[0] * crhs[p] + cscale[1] * cw0[p] + cscale[2] * cw1[p]),
        ),
    )

    for y in range(QC):
        for z in range(QC):
            line = dense(INTERP, [ccor[i * QC * QC + y * QC + z] for i in range(QC)])
            for i in range(QF):
                tmp_a[(i * QC + y) * QC + z] = line[i]
    for x in range(QF):
        for z in range(QC):
            line = dense(INTERP, [tmp_a[(x * QC + i) * QC + z] for i in range(QC)])
            for i in range(QF):
                tmp_b[(x * QF + i) * QC + z] = line[i]
    for x in range(QF):
        for y in range(QF):
            line = dense(INTERP, [tmp_b[(x * QF + y) * QC + i] for i in range(QC)])
            for z in range(QF):
                value = power[(x * QF + y) * QF + z] + line[z]
                for e in range(ex):
                    at = (e * QF + x) * rows_x + y
                    raw[z, pl.ds(at, ey, stride=QF), :] = value[e * ey : (e + 1) * ey]
    crows_x = cor_ref.shape[1] + (-cor_ref.shape[1]) % 8
    for x in range(QC):
        for y in range(QC):
            for z in range(QC):
                value = ccor[(x * QC + y) * QC + z]
                for e in range(ex):
                    at = (e * QC + x) * crows_x + y
                    craw[z, pl.ds(at, ey, stride=QC), :] = value[e * ey : (e + 1) * ey]

    @pl.loop(0, 2)
    def _(c):
        at = pl.multiple_of(c * chunk, 8)
        packed = jnp.concatenate([raw[k, pl.ds(at, chunk), :] for k in range(QF)], axis=1)
        wide[pl.ds(at, chunk), :] = split_dot(packed, back[...])

    for x in range(px):
        out_ref[x] = wide[x * rows_x : x * rows_x + py, :]
    packed = jnp.concatenate([craw[k] for k in range(QC)], axis=1)
    moved = split_dot(packed, cback[...])
    for x in range(cor_ref.shape[0]):
        cor_ref[x] = moved[x * crows_x : x * crows_x + cor_ref.shape[1], :]
    for copy in pending:
        copy.wait_send()


def on_device(nx, ny, source, conductivity, absorption):
    px, py, pz = source.shape
    ex, ey, ez = px // QF, py // QF, pz // QF
    subs = ex * ey
    rows = px * (-(-py // 8) * 8)
    crows = ex * QC * (-(-ey * QC // 8) * 8)
    tiles = -(-(2 * QF * QF + QC * QC) // min(ex, ey))
    f32, bf16 = jnp.float32, jnp.bfloat16
    dirs = len(DIRS)
    longest = max(nx, ny)
    scratch = [
        pltpu.VMEM((3 * rows, pz), f32),
        pltpu.VMEM((QF, 3 * rows, ez), f32),
        pltpu.VMEM((QC, crows, ez), f32),
        pltpu.VMEM((pz, pz), bf16),
        pltpu.VMEM((pz, pz), bf16),
        pltpu.VMEM((QC * ez, QC * ez), bf16),
        pltpu.VMEM((8, QF**3, subs, ez), f32),
        pltpu.VMEM((QF**3, subs, ez), f32),
        pltpu.VMEM((QF**3, subs, ez), f32),
        pltpu.VMEM((8, QC**3, subs, ez), f32),
        pltpu.VMEM((QC**3, subs, ez), f32),
        pltpu.VMEM((QC**3, subs, ez), f32),
        pltpu.VMEM((QF * QF * QC, subs, ez), f32),
        pltpu.VMEM((QF * QF * QC, subs, ez), f32),
        pltpu.VMEM((STAGES, dirs, tiles, subs, ez), f32),
        pltpu.VMEM((STAGES, dirs, tiles, subs, ez), f32),
        pltpu.VMEM((2, 8, ez), f32),
        pltpu.VMEM((2, nx, 8, ez), f32),
        pltpu.VMEM((2, 8, ez), f32),
        pltpu.VMEM((2, ny, 8, ez), f32),
        pltpu.SemaphoreType.DMA((STAGES, dirs)),
        pltpu.SemaphoreType.DMA((STAGES, dirs)),
        pltpu.SemaphoreType.DMA((2, 2, longest)),
        pltpu.SemaphoreType.DMA((2, nx)),
        pltpu.SemaphoreType.DMA((2, ny)),
    ]
    vmem = pl.BlockSpec(memory_space=pltpu.VMEM)
    return pl.pallas_call(
        functools.partial(kernel, nx, ny),
        out_shape=(
            jax.ShapeDtypeStruct(source.shape, f32),
            jax.ShapeDtypeStruct((ex * QC, ey * QC, ez * QC), f32),
        ),
        in_specs=[vmem] * 3,
        out_specs=(vmem, vmem),
        scratch_shapes=scratch,
        compiler_params=pltpu.CompilerParams(
            collective_id=0, has_side_effects=True, vmem_limit_bytes=60 * 1024 * 1024
        ),
    )(source, conductivity, absorption)


def solution(mesh):
    spec = P("gx", "gy", None)
    return jax.shard_map(
        functools.partial(on_device, mesh.shape["gx"], mesh.shape["gy"]),
        mesh=mesh,
        in_specs=(spec,) * 3,
        out_specs=(spec, spec),
        check_vma=False,
    )
```

```python
import functools
import math

import jax
import jax.numpy as jnp
import numpy as np
from jax import lax
from jax.experimental import pallas as pl
from jax.experimental.pallas import tpu as pltpu
from jax.sharding import PartitionSpec as P

SWEEPS = 3
STAGES = 10
MESH = pl.DeviceIdType.MESH
DIRS = [(-1, 0), (1, 0), (0, -1), (0, 1), (-1, -1), (-1, 1), (1, -1), (1, 1)]


def deriv_table(points):
    count = len(points)
    barycentric = np.array(
        [
            1.0 / np.prod([points[j] - points[k] for k in range(count) if k != j])
            for j in range(count)
        ]
    )
    table = np.zeros((count, count))
    for i in range(count):
        for j in range(count):
            if i != j:
                table[i, j] = barycentric[j] / (barycentric[i] * (points[i] - points[j]))
        table[i, i] = -np.sum(table[i])
    return table


ROOT = math.sqrt(3.0 / 7.0)
FINE_POINTS = np.array([-1.0, -ROOT, 0.0, ROOT, 1.0])
FINE_W = np.array([0.1, 49.0 / 90.0, 32.0 / 45.0, 49.0 / 90.0, 0.1])
COARSE_POINTS = np.array([-1.0, 0.0, 1.0])
COARSE_W = np.array([1.0 / 3.0, 4.0 / 3.0, 1.0 / 3.0])
FINE_D = deriv_table(FINE_POINTS)
COARSE_D = deriv_table(COARSE_POINTS)
INTERP = np.stack(
    [
        FINE_POINTS * (FINE_POINTS - 1.0) / 2.0,
        1.0 - FINE_POINTS**2,
        FINE_POINTS * (FINE_POINTS + 1.0) / 2.0,
    ],
    1,
)
RESTRICT = INTERP.T * np.array([0.5, 1.0, 1.0, 1.0, 0.5])[None, :]
QF, QC = 5, 3


def chebyshev_coefficients():
    theta, delta, sigma, rho = 0.75, 0.45, 5.0 / 3.0, 0.6
    x = np.zeros(SWEEPS + 1)
    r = np.zeros(SWEEPS + 1)
    r[0] = 1.0
    d = r / theta
    for sweep in range(SWEEPS):
        x = x + d
        r = r - np.concatenate([[0.0], d[:-1]])
        if sweep + 1 < SWEEPS:
            rho_next = 1.0 / (2.0 * sigma - rho)
            d = rho_next * rho * d + 2.0 * rho_next / delta * r
            rho = rho_next
    return [float(v) for v in x[:SWEEPS]]


CHEB = chebyshev_coefficients()


def antisym(table, u):
    n = len(u)
    half = n // 2
    even = [u[j] + u[n - 1 - j] for j in range(half)]
    odd = [u[j] - u[n - 1 - j] for j in range(half)]
    out = [None] * n
    for i in range(half):
        p = float(table[i, half]) * u[half]
        q = None
        for j in range(half):
            s = (table[i, j] + table[i, n - 1 - j]) / 2
            t = (table[i, j] - table[i, n - 1 - j]) / 2
            p = p + float(s) * even[j]
            q = float(t) * odd[j] if q is None else q + float(t) * odd[j]
        out[i] = q + p
        out[n - 1 - i] = q - p
    mid = None
    for j in range(half):
        term = float(table[half, j]) * odd[j]
        mid = term if mid is None else mid + term
    out[half] = mid
    return out


def dense(table, u):
    out = []
    for i in range(table.shape[0]):
        acc = None
        for j in range(table.shape[1]):
            c = float(table[i, j])
            if abs(c) < 1e-14:
                continue
            term = u[j] if c == 1.0 else c * u[j]
            acc = term if acc is None else acc + term
        out.append(acc)
    return out


def plane_starts(q, axis, a, b):
    strides = (q * q, q, 1)
    other = [s for k, s in enumerate(strides) if k != axis]
    return a * other[0] + b * other[1], strides[axis]


def z_sum(line, lanes):
    lo, hi = line[0], line[-1]
    line[-1] = hi + pltpu.roll(lo, lanes - 1, 1)
    line[0] = lo + pltpu.roll(hi, 1, 1)
    return line


def local_op(src, dst, flux, mass, table, lanes):
    q = table.shape[0]
    for axis in range(3):

        @pl.loop(0, q)
        def _(a, axis=axis):
            def read(b):
                start, step = plane_starts(q, axis, a, b)
                u = [src[start + step * i] for i in range(q)]
                base = None if axis == 0 else [dst[start + step * i] for i in range(q)]
                return u, base

            ahead = read(0)
            for b in range(q):
                u, base = ahead
                if b + 1 < q:
                    ahead = read(b + 1)
                start, step = plane_starts(q, axis, a, b)
                g = antisym(table, u)
                g = [flux[start + step * i] * g[i] for i in range(q)]
                r = antisym(table.T, g)
                for i in range(q):
                    r[i] = (mass[start + step * i] * u[i] if base is None else base[i]) + r[i]
                if axis == 2:
                    r = z_sum(r, lanes)
                for i in range(q):
                    dst[start + step * i] = r[i]


def local_diag(dst, flux, mass, table, lanes):
    q = table.shape[0]
    square = (table * table).T
    for axis in range(3):

        @pl.loop(0, q)
        def _(a, axis=axis):
            for b in range(q):
                start, step = plane_starts(q, axis, a, b)
                r = dense(square, [flux[start + step * i] for i in range(q)])
                for i in range(q):
                    base = mass if axis == 0 else dst
                    r[i] = base[start + step * i] + r[i]
                if axis == 2:
                    r = z_sum(r, lanes)
                for i in range(q):
                    dst[start + step * i] = r[i]


def kernel(
    nx,
    ny,
    src_ref,
    cond_ref,
    abs_ref,
    out_ref,
    cor_ref,
    wide,
    raw,
    craw,
    perm,
    back,
    cback,
    load,
    inv,
    power,
    w0,
    w1,
    w2,
    b,
    power_2,
    flux,
    mass,
    coarse,
    cflux,
    cmass,
    tmp_a,
    tmp_b,
    send,
    recv,
    line_x_send,
    line_x,
    line_y_send,
    line_y,
    send_sem,
    recv_sem,
    line_send_sem,
    line_x_sem,
    line_y_sem,
):
    px, py, pz = src_ref.shape
    ex, ey, ez = px // QF, py // QF, pz // QF
    subs, lanes = ex * ey, ez
    rows_x = -(-py // 8) * 8
    rows = px * rows_x
    mx, my = lax.axis_index("gx"), lax.axis_index("gy")

    def target(dx, dy):
        return (lax.rem(mx + dx + nx, nx), lax.rem(my + dy + ny, ny))

    greeted = {(o, 0) for o in range(1, nx)} | {(0, o) for o in range(1, ny)}
    greeted |= {(dx % nx, dy % ny) for dx, dy in DIRS}
    greeted = sorted(greeted)
    barrier = pltpu.get_barrier_semaphore()
    for dx, dy in greeted:
        pl.semaphore_signal(barrier, inc=1, device_id=target(dx, dy), device_id_type=MESH)

    sub = lax.broadcasted_iota(jnp.int32, (subs, lanes), 0)

    def any_of(indices):
        mask = None
        for index in indices:
            one = sub == index
            mask = one if mask is None else mask | one
        return mask

    x_group = [(sub >= j * ey) & (sub < (j + 1) * ey) for j in range(ex)]
    y_group = [any_of([e * ey + j for e in range(ex)]) for j in range(ey)]
    at_sub = {}

    def single(index):
        if index not in at_sub:
            at_sub[index] = sub == index
        return at_sub[index]

    def shifted(plane, shift):
        shift = shift % subs
        return plane if shift == 0 else pltpu.roll(plane, shift, 0)

    def layout(d):
        dx, dy = DIRS[d]
        if dy == 0:
            return ex, ey, (0 if dx < 0 else ex - 1), (ex - 1 if dx < 0 else 0)
        if dx == 0:
            return ey, 1, (0 if dy < 0 else ey - 1), (ey - 1 if dy < 0 else 0)
        sx, tx = (0, ex - 1) if dx < 0 else (ex - 1, 0)
        sy, ty = (0, ey - 1) if dy < 0 else (ey - 1, 0)
        return subs, 1, sx * ey + sy, tx * ey + ty

    def group_mask(d, j):
        dx, dy = DIRS[d]
        if dy == 0:
            return x_group[j]
        if dx == 0:
            return y_group[j]
        return single(j)

    def face_planes(d, q):
        dx, dy = DIRS[d]
        xs = range(q) if dx == 0 else [0 if dx < 0 else q - 1]
        ys = range(q) if dy == 0 else [0 if dy < 0 else q - 1]
        return [(x * q + y) * q + z for x in xs for y in ys for z in range(q)]

    def copy_of(stage, d, tiles):
        return pltpu.make_async_remote_copy(
            src_ref=send.at[stage, d, pl.ds(0, tiles)],
            dst_ref=recv.at[stage, d, pl.ds(0, tiles)],
            send_sem=send_sem.at[stage, d],
            recv_sem=recv_sem.at[stage, d],
            device_id=target(*DIRS[d]),
            device_id_type=MESH,
        )

    pending = []

    def start_exchange(stage, fields):
        copies = []
        for d in range(len(DIRS)):
            groups, distance, source, _ = layout(d)
            planes = [ref.at[p] for ref, q in fields for p in face_planes(d, q)]
            tiles = -(-len(planes) // groups)
            for t in range(tiles):
                acc = None
                for j, plane in enumerate(planes[t * groups : (t + 1) * groups]):
                    moved = shifted(plane[...], (j - source) * distance)
                    acc = moved if acc is None else jnp.where(group_mask(d, j), moved, acc)
                send[stage, d, t] = acc
            copy = copy_of(stage, d, tiles)
            copy.start()
            copies.append(copy)
        return copies

    not_first_x, not_last_x = sub >= ey, sub < (ex - 1) * ey
    first_y, last_y = y_group[0], y_group[ey - 1]

    def finish_exchange(stage, fields, copies):
        for copy in copies:
            copy.wait_recv()
        pending.extend(copies)

        def received(d, number):
            groups, distance, _, place = layout(d)
            tile, j = divmod(number, groups)
            return shifted(recv[stage, d, tile], (place - j) * distance)

        offsets = [0] * len(DIRS)
        for ref, q in fields:
            last = q - 1
            plane = lambda x, y, z: (x * q + y) * q + z

            def x_sum(lo, hi, from_low, from_high):
                new_lo = lo + jnp.where(not_first_x, shifted(hi, ey), from_low)
                new_hi = hi + jnp.where(not_last_x, shifted(lo, -ey), from_high)
                return new_lo, new_hi

            for y in range(q):
                for z in range(q):
                    number = y * q + z
                    lo, hi = x_sum(
                        ref[plane(0, y, z)],
                        ref[plane(last, y, z)],
                        received(1, offsets[1] + number),
                        received(0, offsets[0] + number),
                    )
                    ref[plane(0, y, z)] = lo
                    ref[plane(last, y, z)] = hi
            for z in range(q):
                low = [received(3, offsets[3] + x * q + z) for x in range(q)]
                high = [received(2, offsets[2] + x * q + z) for x in range(q)]
                low[0], low[last] = x_sum(
                    low[0], low[last], received(7, offsets[7] + z), received(5, offsets[5] + z)
                )
                high[0], high[last] = x_sum(
                    high[0], high[last], received(6, offsets[6] + z), received(4, offsets[4] + z)
                )
                for x in range(q):
                    lo, hi = ref[plane(x, 0, z)], ref[plane(x, last, z)]
                    ref[plane(x, 0, z)] = lo + jnp.where(first_y, low[x], shifted(hi, 1))
                    ref[plane(x, last, z)] = hi + jnp.where(last_y, high[x], shifted(lo, -1))
            for d in range(len(DIRS)):
                offsets[d] += len(face_planes(d, q))

    def start_line(which, along_x, first, second):
        out, slots, sems = (
            (line_x_send, line_x, line_x_sem) if along_x else (line_y_send, line_y, line_y_sem)
        )
        count = nx if along_x else ny
        out[which, 0:1] = first
        out[which, 1:2] = second
        copies = []
        for o in range(1, count):
            copy = pltpu.make_async_remote_copy(
                src_ref=out.at[which],
                dst_ref=slots.at[which, o],
                send_sem=line_send_sem.at[which, 0 if along_x else 1, o],
                recv_sem=sems.at[which, o],
                device_id=target(o, 0) if along_x else target(0, o),
                device_id_type=MESH,
            )
            copy.start()
            copies.append(copy)
        return copies

    def finish_line(which, along_x, copies):
        out, slots = (line_x_send, line_x) if along_x else (line_y_send, line_y)
        count = nx if along_x else ny
        for copy in copies:
            copy.wait_recv()
        pending.extend(copies)
        total = out[which]
        for o in range(1, count):
            total = total + slots[which, o]
        return total[0:1], total[1:2]

    def inverse_estimate(first, second):
        first = jnp.sum(first, axis=1, keepdims=True)
        second = jnp.sum(second, axis=1, keepdims=True)
        return 1.0 / jnp.sqrt(second / (first + 1e-06))

    def coefficients(inv_est):
        power = inv_est
        out = []
        for c in CHEB:
            out.append(jnp.broadcast_to(c * power, (subs, lanes)))
            power = power * inv_est
        return out

    for k in range(QF):
        row = lax.broadcasted_iota(jnp.int32, (pz, ez), 0)
        col = lax.broadcasted_iota(jnp.int32, (pz, ez), 1)
        perm[:, k * ez : (k + 1) * ez] = jnp.where(row == QF * col + k, 1.0, 0.0).astype(
            jnp.bfloat16
        )

    def transposed_permutation(ref, q):
        for k in range(q):
            row = lax.broadcasted_iota(jnp.int32, (ez, q * ez), 0)
            col = lax.broadcasted_iota(jnp.int32, (ez, q * ez), 1)
            ref[k * ez : (k + 1) * ez, :] = jnp.where(col == q * row + k, 1.0, 0.0).astype(
                jnp.bfloat16
            )

    def split_dot(value, table):
        high = value.astype(jnp.bfloat16)
        rest = value - high.astype(jnp.float32)
        mid = rest.astype(jnp.bfloat16)
        low = (rest - mid.astype(jnp.float32)).astype(jnp.bfloat16)
        dot = functools.partial(jnp.dot, preferred_element_type=jnp.float32)
        return dot(high, table) + (dot(mid, table) + dot(low, table))

    for n, ref in enumerate((src_ref, cond_ref, abs_ref)):
        for x in range(px):
            wide[n * rows + x * rows_x : n * rows + x * rows_x + py, :] = ref[x]
    chunk = rows // 2

    @pl.loop(0, 6)
    def _(c):
        at = pl.multiple_of(c * chunk, 8)
        moved = split_dot(wide[pl.ds(at, chunk), :], perm[...])
        for k in range(QF):
            raw[k, pl.ds(at, chunk), :] = moved[:, k * ez : (k + 1) * ez]

    pick = {0: 0, 2: 1, 4: 2}
    for x in range(QF):
        for y in range(QF):
            for z in range(QF):
                p = (x * QF + y) * QF + z
                weight = float(FINE_W[x] * FINE_W[y] * FINE_W[z])
                on_coarse = x in pick and y in pick and z in pick
                for e in range(ex):
                    at = (e * QF + x) * rows_x + y
                    values = [
                        raw[z, pl.ds(n * rows + at, ey, stride=QF), :] for n in range(3)
                    ]
                    place = slice(e * ey, (e + 1) * ey)
                    load[p, place, :] = weight * values[0]
                    flux[p, place, :] = weight * values[1]
                    mass[p, place, :] = weight * values[2]
                    if on_coarse:
                        i, j, k = pick[x], pick[y], pick[z]
                        cp = (i * QC + j) * QC + k
                        cw = float(COARSE_W[i] * COARSE_W[j] * COARSE_W[k])
                        cflux[cp, place, :] = cw * values[1]
                        cmass[cp, place, :] = cw * values[2]

    cinv, cur, crhs, cw0, cb, cpow, cw1, ccor = [coarse.at[i] for i in range(8)]

    def each(q, body):
        @pl.loop(0, q * q)
        def _(a):
            for i in range(q):
                body(a * q + i)

    def squares(q, values):
        def body(a, acc):
            for i in range(q):
                v = values(a * q + i)
                acc = acc + v * v
            return acc

        total = lax.fori_loop(0, q * q, body, jnp.zeros((subs, lanes), jnp.float32))
        return jnp.sum(total, axis=0, keepdims=True)

    def store(dst, values):
        def body(p):
            dst[p] = values(p)

        return body

    def restrict(field, dst):
        if True:

            @pl.loop(0, QF)
            def _(a):
                for c in range(QF):
                    line = dense(RESTRICT, [field[i * QF * QF + a * QF + c] for i in range(QF)])
                    for i in range(QC):
                        tmp_a[i * QF * QF + a * QF + c] = line[i]

        @pl.loop(0, QC)
        def _(a):
            for c in range(QF):
                line = dense(RESTRICT, [tmp_a[a * QF * QF + i * QF + c] for i in range(QF)])
                for i in range(QC):
                    tmp_b[a * QC * QF + i * QF + c] = line[i]

        @pl.loop(0, QC)
        def _(a):
            for c in range(QC):
                line = dense(RESTRICT, [tmp_b[a * QC * QF + c * QF + i] for i in range(QF)])
                line = z_sum(line, lanes)
                for i in range(QC):
                    dst[a * QC * QC + c * QC + i] = line[i]

    def apply_fine(src, dst):
        local_op(src, dst, flux, mass, FINE_D, lanes)

    def apply_coarse(src, dst):
        local_op(src, dst, cflux, cmass, COARSE_D, lanes)

    @pl.loop(0, QF * QF)
    def _(a):
        line = z_sum([load[a * QF + i] for i in range(QF)], lanes)
        load[a * QF] = line[0]
        load[a * QF + QF - 1] = line[-1]

    pl.semaphore_wait(barrier, len(greeted))
    load_fields = [(load, QF)]
    load_copies = start_exchange(7, load_fields)
    local_diag(inv, flux, mass, FINE_D, lanes)
    local_diag(cinv, cflux, cmass, COARSE_D, lanes)
    fields = [(inv, QF), (cinv, QC)]
    copies = start_exchange(0, fields)
    finish_exchange(7, load_fields, load_copies)

    apply_fine(load, power)
    power_fields = [(power, QF)]
    power_copies = start_exchange(8, power_fields)
    finish_exchange(0, fields, copies)

    def invert(p):
        value = 1.0 / inv[p]
        inv[p] = value
        b[p] = value * load[p]

    each(QF, invert)
    each(QC, store(cinv, lambda p: 1.0 / cinv[p]))
    restrict(load, crhs)
    apply_fine(b, w0)
    fields = [(w0, QF), (crhs, QC)]
    copies = start_exchange(1, fields)

    finish_exchange(8, power_fields, power_copies)
    each(QF, store(power, lambda p: inv[p] * power[p]))
    apply_fine(power, power_2)
    power_fields = [(power_2, QF)]
    power_copies = start_exchange(9, power_fields)
    sum_first = squares(QF, lambda p: power[p])

    finish_exchange(1, fields, copies)
    each(QF, store(b, lambda p: inv[p] * w0[p]))
    apply_coarse(crhs, cpow)
    apply_fine(b, w1)
    fields = [(w1, QF), (cpow, QC)]
    copies = start_exchange(2, fields)
    finish_exchange(9, power_fields, power_copies)
    sum_second = squares(QF, lambda p: inv[p] * power_2[p])
    line = start_line(0, True, sum_first, sum_second)
    transposed_permutation(back, QF)
    transposed_permutation(cback, QC)
    finish_exchange(2, fields, copies)
    each(QF, store(b, lambda p: inv[p] * w1[p]))
    each(QC, store(cpow, lambda p: cinv[p] * cpow[p]))

    apply_fine(b, w2)
    line = start_line(0, False, *finish_line(0, True, line))
    apply_coarse(cpow, cur)
    fields = [(w2, QF), (cur, QC)]
    copies = start_exchange(3, fields)
    csum_first = squares(QC, lambda p: cpow[p])
    scale = coefficients(inverse_estimate(*finish_line(0, False, line)))
    finish_exchange(3, fields, copies)
    csum_second = squares(QC, lambda p: cinv[p] * cur[p])
    each(
        QF,
        store(
            b, lambda p: load[p] - (scale[0] * w0[p] + scale[1] * w1[p] + scale[2] * w2[p])
        ),
    )

    restrict(b, crhs)
    fields = [(crhs, QC)]
    copies = start_exchange(4, fields)
    line = start_line(1, True, csum_first, csum_second)
    each(
        QF,
        store(
            power,
            lambda p: inv[p] * (scale[0] * load[p] + scale[1] * w0[p] + scale[2] * w1[p]),
        ),
    )
    finish_exchange(4, fields, copies)
    each(QC, store(cb, lambda p: cinv[p] * crhs[p]))

    apply_coarse(cb, cw0)
    fields = [(cw0, QC)]
    copies = start_exchange(5, fields)
    line = start_line(1, False, *finish_line(1, True, line))
    finish_exchange(5, fields, copies)
    each(QC, store(cb, lambda p: cinv[p] * cw0[p]))

    apply_coarse(cb, cw1)
    fields = [(cw1, QC)]
    copies = start_exchange(6, fields)
    cscale = coefficients(inverse_estimate(*finish_line(1, False, line)))
    finish_exchange(6, fields, copies)
    each(
        QC,
        store(
            ccor,
            lambda p: cinv[p]
            * (cscale[0] * crhs[p] + cscale[1] * cw0[p] + cscale[2] * cw1[p]),
        ),
    )

    for y in range(QC):
        for z in range(QC):
            line = dense(INTERP, [ccor[i * QC * QC + y * QC + z] for i in range(QC)])
            for i in range(QF):
                tmp_a[(i * QC + y) * QC + z] = line[i]
    for x in range(QF):
        for z in range(QC):
            line = dense(INTERP, [tmp_a[(x * QC + i) * QC + z] for i in range(QC)])
            for i in range(QF):
                tmp_b[(x * QF + i) * QC + z] = line[i]
    for x in range(QF):
        for y in range(QF):
            line = dense(INTERP, [tmp_b[(x * QF + y) * QC + i] for i in range(QC)])
            for z in range(QF):
                value = power[(x * QF + y) * QF + z] + line[z]
                for e in range(ex):
                    at = (e * QF + x) * rows_x + y
                    raw[z, pl.ds(at, ey, stride=QF), :] = value[e * ey : (e + 1) * ey]
    crows_x = cor_ref.shape[1] + (-cor_ref.shape[1]) % 8
    for x in range(QC):
        for y in range(QC):
            for z in range(QC):
                value = ccor[(x * QC + y) * QC + z]
                for e in range(ex):
                    at = (e * QC + x) * crows_x + y
                    craw[z, pl.ds(at, ey, stride=QC), :] = value[e * ey : (e + 1) * ey]

    @pl.loop(0, 2)
    def _(c):
        at = pl.multiple_of(c * chunk, 8)
        packed = jnp.concatenate([raw[k, pl.ds(at, chunk), :] for k in range(QF)], axis=1)
        wide[pl.ds(at, chunk), :] = split_dot(packed, back[...])

    for x in range(px):
        out_ref[x] = wide[x * rows_x : x * rows_x + py, :]
    packed = jnp.concatenate([craw[k] for k in range(QC)], axis=1)
    moved = split_dot(packed, cback[...])
    for x in range(cor_ref.shape[0]):
        cor_ref[x] = moved[x * crows_x : x * crows_x + cor_ref.shape[1], :]
    for copy in pending:
        copy.wait_send()


def on_device(nx, ny, source, conductivity, absorption):
    px, py, pz = source.shape
    ex, ey, ez = px // QF, py // QF, pz // QF
    subs = ex * ey
    rows = px * (-(-py // 8) * 8)
    crows = ex * QC * (-(-ey * QC // 8) * 8)
    tiles = -(-(QF * QF + QC * QC) // min(ex, ey))
    f32, bf16 = jnp.float32, jnp.bfloat16
    dirs = len(DIRS)
    longest = max(nx, ny)
    scratch = [
        pltpu.VMEM((3 * rows, pz), f32),
        pltpu.VMEM((QF, 3 * rows, ez), f32),
        pltpu.VMEM((QC, crows, ez), f32),
        pltpu.VMEM((pz, pz), bf16),
        pltpu.VMEM((pz, pz), bf16),
        pltpu.VMEM((QC * ez, QC * ez), bf16),
        *[pltpu.VMEM((QF**3, subs, ez), f32)] * 8,
        pltpu.VMEM((QF**3, subs, ez), f32),
        pltpu.VMEM((QF**3, subs, ez), f32),
        pltpu.VMEM((8, QC**3, subs, ez), f32),
        pltpu.VMEM((QC**3, subs, ez), f32),
        pltpu.VMEM((QC**3, subs, ez), f32),
        pltpu.VMEM((QF * QF * QC, subs, ez), f32),
        pltpu.VMEM((QF * QF * QC, subs, ez), f32),
        pltpu.VMEM((STAGES, dirs, tiles, subs, ez), f32),
        pltpu.VMEM((STAGES, dirs, tiles, subs, ez), f32),
        pltpu.VMEM((2, 8, ez), f32),
        pltpu.VMEM((2, nx, 8, ez), f32),
        pltpu.VMEM((2, 8, ez), f32),
        pltpu.VMEM((2, ny, 8, ez), f32),
        pltpu.SemaphoreType.DMA((STAGES, dirs)),
        pltpu.SemaphoreType.DMA((STAGES, dirs)),
        pltpu.SemaphoreType.DMA((2, 2, longest)),
        pltpu.SemaphoreType.DMA((2, nx)),
        pltpu.SemaphoreType.DMA((2, ny)),
    ]
    vmem = pl.BlockSpec(memory_space=pltpu.VMEM)
    return pl.pallas_call(
        functools.partial(kernel, nx, ny),
        out_shape=(
            jax.ShapeDtypeStruct(source.shape, f32),
            jax.ShapeDtypeStruct((ex * QC, ey * QC, ez * QC), f32),
        ),
        in_specs=[vmem] * 3,
        out_specs=(vmem, vmem),
        scratch_shapes=scratch,
        compiler_params=pltpu.CompilerParams(
            collective_id=0, has_side_effects=True, vmem_limit_bytes=60 * 1024 * 1024
        ),
    )(source, conductivity, absorption)


def solution(mesh):
    spec = P("gx", "gy", None)
    return jax.shard_map(
        functools.partial(on_device, mesh.shape["gx"], mesh.shape["gy"]),
        mesh=mesh,
        in_specs=(spec,) * 3,
        out_specs=(spec, spec),
        check_vma=False,
    )
```
